32 devices in a mesh: row: 2 (over x), col: 16 (over z, y, core).
Axes of the slice: x: 2, y: 2, z: 4, core: 2. Of those that a mesh axis runs over, the one named last changes fastest.
Arguments:
- pair_state: bfloat16 [256, 256, 256], P('row', 'col'), may hold values from -6 to 6
- residue_mask: int32 [256], replicated, may hold values 0 or 1
- chain_ids: int32 [256], replicated, may hold values from 0 to 3, never falling along the last dimension, each value on 1 to 128 neighbouring positions
- gain_transition: float32 [256], replicated, may hold values from 0.1 to 1.9
- hidden_weight: bfloat16 [256, 1024], replicated, may hold values from -0.375 to 0.375
- out_weight: bfloat16 [1024, 256], replicated, may hold values from -0.1875 to 0.1875
- gain_attention: float32 [256], replicated, may hold values from 0.1 to 1.9
- query_weight: bfloat16 [256, 256], replicated, may hold values from -4 to 4
- key_weight: bfloat16 [256, 256], replicated, may hold values from -4 to 4
- value_weight: bfloat16 [256, 256], replicated, may hold values from -0.375 to 0.375
- gate_weight: bfloat16 [256, 256], replicated, may hold values from -0.375 to 0.375
- bias_weight: bfloat16 [256, 8], replicated, may hold values from -0.375 to 0.375
- chain_weight: float32 [8], replicated, may hold values from -2 to 2
- output_weight: bfloat16 [256, 256], replicated, may hold values from -4 to 4
Outputs:
- symmetric_pair: bfloat16 [256, 256, 256], P('row', 'col')
The draws below stay inside these ranges and needn't reach their ends.
All inputs are finite; a program needn't handle non-finite values.
Results may differ from the reference program's by a relative error of at most 0.004.
The reference program's roundings to bfloat16 on the way (of `first_norm`, `hidden_act`, `normed`, `pair_bias`, `attn_weights`, `gated` and `update`) count: a program that leaves them out, or rounds other values in their place, can miss the bound.
Values may be sent and summed in bfloat16 or wider, within the bound.
A program may use at most 128 MiB of HBM per device.

```python
import math
import jax
import jax.numpy as jnp
import numpy as np
from jax import lax

PAIR_DIM = 256
HIDDEN_DIM = 1024
HEADS = 8
HEAD_DIM = 32
LENGTH = 256


def draw_query_weight(key, part):
    drawn = jax.random.normal(jax.random.fold_in(key, 21), (PAIR_DIM, HEADS * HEAD_DIM), jnp.float32) / math.sqrt(PAIR_DIM)
    return jnp.clip(drawn, -4.0, 4.0).astype(jnp.bfloat16)


def draw_key_weight(key, part):
    drawn = jax.random.normal(jax.random.fold_in(key, 23), (PAIR_DIM, HEADS * HEAD_DIM), jnp.float32) / math.sqrt(PAIR_DIM)
    return jnp.clip(drawn, -4.0, 4.0).astype(jnp.bfloat16)


def set_ends(values, stream_key, least, top_value):
    place = [jax.random.randint(jax.random.fold_in(stream_key, axis), (), 0, length) for axis, length in enumerate(values.shape)]
    longest = values.shape.index(max(values.shape))
    next_to = place[:longest] + [(place[longest] + 1) % values.shape[longest]] + place[longest + 1:]
    return values.at[tuple(place)].set(least).at[tuple(next_to)].set(top_value)


def block_levels(own_key, extent, shards, low, top_value):
    loudness, own = 1.0, jax.random.fold_in(own_key, 6)
    for dim, blocks in shards:
        heights = jnp.exp(jax.random.uniform(jax.random.fold_in(own, dim), (blocks,), jnp.float32, low / len(shards), top_value / len(shards)))
        loudness = loudness * jnp.repeat(heights, extent[dim] // blocks).reshape([-1 if axis == dim else 1 for axis in range(len(extent))])
    return loudness


def profile(amount, total, limit, lean):
    weights = [(1 << 20) // math.isqrt(rank ** lean) + 1 for rank in range(2, amount + 1)]
    spare, holding = total - limit - (amount - 1), [1] * (amount - 1)
    while spare > 0:
        candidates = [i for i in range(amount - 1) if holding[i] < limit]
        pool, budget = sum([weights[i] for i in candidates]), spare
        for i in candidates:
            extra = min(limit - holding[i], max(1, budget * weights[i] // pool), spare)
            holding[i] = holding[i] + extra
            spare = spare - extra
    return np.array([limit] + holding)


def uneven_parts(key, amount, total, bound, slope):
    if amount == 2:
        one = jax.random.randint(key, (), max(1, total - bound), min(bound, total - 1) + 1)
        return jnp.stack([one, total - one])
    tallies = jnp.asarray(profile(amount, total, bound, slope), jnp.int32)
    couples = (amount - 1) // 2
    source_of, receiver = tallies[1:1 + 2 * couples:2], tallies[2:2 + 2 * couples:2]
    slack = jnp.minimum(source_of - 1, bound - receiver)
    moved = jax.random.randint(jax.random.fold_in(key, 1), (couples,), 0, 1 << 20) % (slack + 1)
    tallies = tallies.at[1:1 + 2 * couples:2].set(source_of - moved).at[2:2 + 2 * couples:2].set(receiver + moved)
    return tallies[jax.random.permutation(jax.random.fold_in(key, 2), amount)]


def bell_draw(stream_key, extent, spread, reach, cuts=(), kind=jnp.bfloat16):
    entries = spread * jax.random.normal(stream_key, extent, jnp.float32)
    if cuts:
        entries = entries * block_levels(stream_key, extent, cuts, -0.22, 0.18)
    return jnp.clip(entries, -reach, reach).astype(kind)


def setup_inputs(seed: int = 0) -> dict:
    seeds = jax.random.split(jax.random.key(seed), 15)
    return {
        "pair_state": bell_draw(seeds[0], (LENGTH, LENGTH, PAIR_DIM), 1.0, 6.0, ((0, 2), (1, 16))),
        "residue_mask": set_ends((jax.random.randint(seeds[1], (LENGTH,), 0, 4) < 3).astype(jnp.int32), jax.random.fold_in(seeds[1], 1), 0, 1),
        "chain_ids": jnp.searchsorted(jnp.cumsum(uneven_parts(seeds[2], 4, LENGTH, LENGTH // 2, 0)), jnp.arange(LENGTH), side="right").astype(jnp.int32),
        "gain_transition": jnp.clip(1.0 + 0.18 * jax.random.normal(seeds[3], (PAIR_DIM,), jnp.float32), 0.1, 1.9),
        "hidden_weight": bell_draw(seeds[4], (PAIR_DIM, HIDDEN_DIM), PAIR_DIM ** -0.5, 0.375),
        "out_weight": bell_draw(seeds[5], (HIDDEN_DIM, PAIR_DIM), HIDDEN_DIM ** -0.5, 0.1875),
        "gain_attention": jnp.clip(1.0 + 0.18 * jax.random.normal(seeds[6], (PAIR_DIM,), jnp.float32), 0.1, 1.9),
        "query_weight": draw_query_weight(jax.random.fold_in(seeds[14], 71), 0),
        "key_weight": draw_key_weight(jax.random.fold_in(seeds[14], 71), 0),
        "value_weight": bell_draw(seeds[9], (PAIR_DIM, HEADS * HEAD_DIM), PAIR_DIM ** -0.5, 0.375),
        "gate_weight": bell_draw(seeds[10], (PAIR_DIM, HEADS * HEAD_DIM), PAIR_DIM ** -0.5, 0.375),
        "bias_weight": bell_draw(seeds[11], (PAIR_DIM, HEADS), PAIR_DIM ** -0.5, 0.375),
        "chain_weight": jnp.clip(jax.random.uniform(seeds[12], (HEADS,), jnp.float32, -2.0, 2.0), -2.0, 2.0),
        "output_weight": bell_draw(seeds[13], (HEADS * HEAD_DIM, PAIR_DIM), 0.25, 4.0),
    }


mask_penalty = 1000000000.0
norm_epsilon = 1e-05

def normalize(values, gain):
    center = values - lax.optimization_barrier(jnp.mean(values, axis=-1, keepdims=True))
    variance = lax.optimization_barrier(jnp.mean(center * center, axis=-1, keepdims=True))
    return center * lax.rsqrt(variance + norm_epsilon) * gain

def reference(pair_state, residue_mask, chain_ids, gain_transition, hidden_weight, out_weight, gain_attention, query_weight, key_weight, value_weight, gate_weight, bias_weight, chain_weight, output_weight):
    length = pair_state.shape[0]
    head_count = chain_weight.shape[0]
    head_dim = query_weight.shape[1] // head_count
    score_scale = 1.0 / math.sqrt(head_dim)
    positions = jnp.arange(length, dtype=jnp.int32)

    def transition_row(position):
        sym_row = pair_state[position].astype(jnp.float32) + pair_state[:, position].astype(jnp.float32)
        first_norm = normalize(sym_row, gain_transition).astype(jnp.bfloat16)
        hidden_act = jax.nn.relu(jnp.dot(first_norm, hidden_weight, preferred_element_type=jnp.float32)).astype(jnp.bfloat16)
        carried_row = sym_row + jnp.dot(hidden_act, out_weight, preferred_element_type=jnp.float32)
        normed_row = normalize(carried_row, gain_attention).astype(jnp.bfloat16)
        return (carried_row, normed_row)
    carried, normed = lax.map(transition_row, positions)

    def bias_row(normed_row):
        return jnp.dot(normed_row, bias_weight, preferred_element_type=jnp.float32).astype(jnp.bfloat16)
    pair_bias = jnp.transpose(lax.map(bias_row, normed), (2, 0, 1)).astype(jnp.float32)
    same_chain = (chain_ids[:, None] == chain_ids[None, :]).astype(jnp.float32)
    penalty = mask_penalty * (1 - residue_mask).astype(jnp.float32)
    full_bias = pair_bias + chain_weight[:, None, None] * same_chain[None] - penalty[None, None, :]

    def attend_row(normed_row):
        query_rows = jnp.dot(normed_row, query_weight, preferred_element_type=jnp.float32).astype(jnp.bfloat16).reshape(length, head_count, head_dim)
        key_rows = jnp.dot(normed_row, key_weight, preferred_element_type=jnp.float32).astype(jnp.bfloat16).reshape(length, head_count, head_dim)
        value_rows = jnp.dot(normed_row, value_weight, preferred_element_type=jnp.float32).astype(jnp.bfloat16).reshape(length, head_count, head_dim)
        gate_vals = jax.nn.sigmoid(jnp.dot(normed_row, gate_weight, preferred_element_type=jnp.float32))
        scores = jnp.einsum('jhd,khd->hjk', query_rows.astype(jnp.float32), key_rows.astype(jnp.float32)) * score_scale + full_bias
        row_max = lax.optimization_barrier(jnp.max(scores, axis=-1, keepdims=True))
        exponent = jnp.exp(scores - row_max)
        attn_weights = (exponent / lax.optimization_barrier(jnp.sum(exponent, axis=-1, keepdims=True))).astype(jnp.bfloat16)
        mixture = jnp.einsum('hjk,khd->jhd', attn_weights.astype(jnp.float32), value_rows.astype(jnp.float32)).reshape(length, head_count * head_dim)
        gated = (gate_vals * mixture).astype(jnp.bfloat16)
        return jnp.dot(gated, output_weight, preferred_element_type=jnp.float32).astype(jnp.bfloat16)
    update = lax.map(attend_row, normed)
    layer_out = carried + update.astype(jnp.float32)
    return (layer_out + jnp.swapaxes(layer_out, 0, 1)).astype(jnp.bfloat16)
```

```python
import functools
import math

import jax
import jax.numpy as jnp
from jax import lax
from jax.experimental import pallas as pl
from jax.experimental.pallas import tpu as pltpu
from jax.sharding import PartitionSpec as P

MESH = pl.DeviceIdType.MESH
VMEM_LIMIT = 60 * 1024 * 1024
LOG2_E = math.log2(math.e)
PARTS = 4
LANES = 128

mask_penalty = 1000000000.0
norm_epsilon = 1e-05


def normalize(values, gain):
    center = values - jnp.mean(values, axis=-1, keepdims=True)
    variance = jnp.mean(center * center, axis=-1, keepdims=True)
    return center * lax.rsqrt(variance + norm_epsilon) * gain


def mirror(tile):
    tile_rows, tile_cols, channels = tile.shape
    col_count = lax.axis_size("col")
    row_count = lax.axis_size("row")
    col_ratio = col_count // row_count
    piece_len = tile_cols * tile_cols // col_count
    sectioned = tile.reshape(col_ratio, col_count, piece_len, channels)
    sectioned = lax.all_to_all(sectioned, "col", split_axis=1, concat_axis=1, tiled=True)
    sectioned = sectioned.reshape(col_ratio, row_count, col_ratio, piece_len, channels)
    sectioned = lax.all_to_all(sectioned, "row", split_axis=1, concat_axis=1, tiled=True)
    sectioned = jnp.transpose(sectioned, (1, 0, 2, 3, 4)).reshape(
        col_count, col_ratio, piece_len, channels
    )
    sectioned = lax.all_to_all(sectioned, "col", split_axis=0, concat_axis=0, tiled=True)
    sectioned = jnp.transpose(sectioned, (1, 0, 2, 3)).reshape(
        col_ratio, tile_cols, tile_cols, channels
    )
    return jnp.transpose(sectioned, (0, 2, 1, 3)).reshape(tile_rows, tile_cols, channels)


def attend(query_part, gate_part, key_part, value_part, bias_part, head_count, output_weight):
    query_total = query_part.shape[0]
    key_total = key_part.shape[0]
    head_dim = query_part.shape[1] // head_count
    score_scale = 1.0 / math.sqrt(head_dim)
    query_heads = query_part.reshape(query_total, head_count, head_dim)
    key_heads = key_part.reshape(key_total, head_count, head_dim)
    value_heads = value_part.reshape(key_total, head_count, head_dim)
    scores = (
        jnp.einsum("jhd,khd->hjk", query_heads, key_heads, preferred_element_type=jnp.float32)
        * score_scale
        + bias_part
    )
    row_max = jnp.max(scores, axis=-1, keepdims=True)
    exponent = jnp.exp(scores - row_max)
    attn_weights = (exponent / jnp.sum(exponent, axis=-1, keepdims=True)).astype(jnp.bfloat16)
    mixture = jnp.einsum(
        "hjk,khd->jhd", attn_weights, value_heads, preferred_element_type=jnp.float32
    )
    gated = (gate_part * mixture.reshape(query_total, head_count * head_dim)).astype(jnp.bfloat16)
    return jnp.dot(gated, output_weight, preferred_element_type=jnp.float32).astype(jnp.bfloat16)


def mirror_layout(
    normed_tile,
    bias_tile,
    chain_ids,
    penalty,
    chain_weight,
    query_weight,
    key_weight,
    value_weight,
    gate_weight,
    output_weight,
):
    tile_rows, tile_cols, channels = normed_tile.shape
    head_count = bias_tile.shape[0]
    row_start = lax.axis_index("row") * tile_rows
    flat_tile = normed_tile.reshape(tile_rows * tile_cols, channels)
    key_tile = (
        jnp.dot(flat_tile, key_weight, preferred_element_type=jnp.float32)
        .astype(jnp.bfloat16)
        .reshape(tile_rows, tile_cols, -1)
    )
    value_tile = (
        jnp.dot(flat_tile, value_weight, preferred_element_type=jnp.float32)
        .astype(jnp.bfloat16)
        .reshape(tile_rows, tile_cols, -1)
    )
    key_all, value_all = (
        lax.all_gather(key_tile, "row", axis=0, tiled=True),
        lax.all_gather(value_tile, "row", axis=0, tiled=True),
    )
    bias_rows = lax.all_gather(bias_tile, "col", axis=2, tiled=True)
    chain_rows = lax.dynamic_slice_in_dim(chain_ids, row_start, tile_rows, 0)
    same_chain = (chain_rows[:, None] == chain_ids[None, :]).astype(jnp.float32)
    bias_full = (
        bias_rows.astype(jnp.float32)
        + chain_weight[:, None, None] * same_chain[None]
        - penalty[None, None, :]
    )
    query_tile = (
        jnp.dot(flat_tile, query_weight, preferred_element_type=jnp.float32)
        .astype(jnp.bfloat16)
        .reshape(tile_rows, tile_cols, -1)
    )
    gate_tile = jax.nn.sigmoid(
        jnp.dot(flat_tile, gate_weight, preferred_element_type=jnp.float32)
    ).reshape(tile_rows, tile_cols, -1)

    def one_column(position):
        query_part = lax.dynamic_index_in_dim(query_tile, position, 1, keepdims=False)
        gate_part = lax.dynamic_index_in_dim(gate_tile, position, 1, keepdims=False)
        key_part = lax.dynamic_index_in_dim(key_all, position, 1, keepdims=False)
        value_part = lax.dynamic_index_in_dim(value_all, position, 1, keepdims=False)
        return attend(
            query_part, gate_part, key_part, value_part, bias_full, head_count, output_weight
        )

    results = lax.map(one_column, jnp.arange(tile_cols, dtype=jnp.int32))
    return jnp.transpose(results, (1, 0, 2))


def tile_layout(
    pair_state,
    residue_mask,
    chain_ids,
    gain_transition,
    hidden_weight,
    out_weight,
    gain_attention,
    query_weight,
    key_weight,
    value_weight,
    gate_weight,
    bias_weight,
    chain_weight,
    output_weight,
):
    tile_rows, tile_cols, channels = pair_state.shape
    head_count = chain_weight.shape[0]
    mirrored = mirror(pair_state)
    sym_tile = pair_state.astype(jnp.float32) + mirrored.astype(jnp.float32)
    flat_sym = sym_tile.reshape(tile_rows * tile_cols, channels)
    first_norm = normalize(flat_sym, gain_transition).astype(jnp.bfloat16)
    hidden_act = jax.nn.relu(
        jnp.dot(first_norm, hidden_weight, preferred_element_type=jnp.float32)
    ).astype(jnp.bfloat16)
    carried = flat_sym + jnp.dot(hidden_act, out_weight, preferred_element_type=jnp.float32)
    normed = normalize(carried, gain_attention).astype(jnp.bfloat16)
    bias_tile = (
        jnp.einsum("pd,dh->hp", normed, bias_weight, preferred_element_type=jnp.float32)
        .astype(jnp.bfloat16)
        .reshape(head_count, tile_rows, tile_cols)
    )
    penalty = mask_penalty * (1 - residue_mask).astype(jnp.float32)
    normed_tile = normed.reshape(tile_rows, tile_cols, channels)
    arguments = (
        normed_tile,
        bias_tile,
        chain_ids,
        penalty,
        chain_weight,
        query_weight,
        key_weight,
        value_weight,
        gate_weight,
        output_weight,
    )
    own_update = mirror_layout(*arguments)
    other_update = mirror(own_update)
    total = (
        2.0 * carried.reshape(tile_rows, tile_cols, channels)
        + own_update.astype(jnp.float32)
        + other_update.astype(jnp.float32)
    )
    return total.astype(jnp.bfloat16)


def greet_all(row_count, col_count):
    device_total = row_count * col_count
    me = lax.axis_index("col") * row_count + lax.axis_index("row")
    barrier = pltpu.get_barrier_semaphore()

    def greet(step, carry):
        peer = lax.rem(me + step, device_total)
        pl.semaphore_signal(
            barrier,
            inc=1,
            device_id=(lax.rem(peer, row_count), peer // row_count),
            device_id_type=MESH,
        )
        return carry

    lax.fori_loop(1, device_total, greet, 0)
    pl.semaphore_wait(barrier, device_total - 1)


def layer_kernel(
    row_count,
    col_count,
    tile_ref,
    turned_ref,
    mask_ref,
    chain_ref,
    gain_transition_ref,
    hidden_weight_ref,
    out_weight_ref,
    gain_attention_ref,
    query_weight_ref,
    key_weight_ref,
    value_weight_ref,
    gate_weight_ref,
    bias_weight_ref,
    chain_weight_ref,
    output_weight_ref,
    out_ref,
    row_buf,
    col_buf,
    relay_buf,
    bias_buf,
    same_buf,
    penalty_buf,
    bias_full,
    carried_buf,
    normed_buf,
    key_buf,
    query_buf,
    value_buf,
    gate_buf,
    query_turned,
    value_turned,
    gate_turned,
    score_buf,
    weight_buf,
    update_buf,
    recv_buf,
    turned,
    sum_buf,
    relay_send,
    relay_recv,
    row_send,
    row_recv,
    col_send,
    col_recv,
    bias_send,
    bias_recv,
    pair_send,
    pair_recv,
    update_send,
    update_recv,
    sum_send,
    sum_recv,
):
    span, _, own, tile_cols, channels = tile_ref.shape
    parts, _, rows_in_part = relay_buf.shape[:3]
    length = row_buf.shape[1]
    tile_rows = length // row_count
    head_count = bias_weight_ref.shape[0]
    inner_total = key_weight_ref.shape[1]
    head_dim = inner_total // head_count
    score_scale = LOG2_E / math.sqrt(head_dim)
    device_total = row_count * col_count
    chip_total = device_total // 2
    row_id, col_id = lax.axis_index("row"), lax.axis_index("col")
    other_row = 1 - row_id
    me = col_id * row_count + row_id
    side = lax.rem(col_id, 2)
    pair = col_id // 2
    chip = pair * row_count + row_id
    lane_blocks = [slice(start, start + LANES) for start in range(0, channels, LANES)]

    def loop(first, last, body):
        def one(step, carry):
            body(step)
            return carry

        lax.fori_loop(first, last, one, 0)

    def await_bytes(like, semaphore):
        pltpu.make_async_copy(like, like, semaphore).wait()

    def rows_of(part):
        return pl.ds(part * rows_in_part, rows_in_part)

    def relay_copy(part):
        return pltpu.make_async_remote_copy(
            src_ref=tile_ref.at[:, other_row, rows_of(part)],
            dst_ref=relay_buf.at[part],
            send_sem=relay_send.at[part],
            recv_sem=relay_recv.at[part],
            device_id=(other_row, col_id),
            device_id_type=MESH,
        )

    def start_rows(origin, slot, part, source):
        target = origin * span + slot
        columns = pl.ds(pl.multiple_of(col_id * tile_cols, tile_cols), tile_cols)
        landing = row_buf.at[rows_of(part), columns, :]

        @pl.when(target != col_id)
        def _():
            pltpu.make_async_remote_copy(
                src_ref=source,
                dst_ref=landing,
                send_sem=row_send,
                recv_sem=row_recv.at[part],
                device_id=(row_id, target),
                device_id_type=MESH,
            ).start()

        @pl.when(target == col_id)
        def _():
            pltpu.make_async_copy(source, landing, row_recv.at[part]).start()

    def over_slots(body):
        loop(0, span, lambda step: body(lax.rem(col_id + step, span)))

    def direct(part):
        over_slots(
            lambda slot: start_rows(row_id, slot, part, tile_ref.at[slot, row_id, rows_of(part)])
        )

    def pass_on(part):
        await_bytes(relay_buf.at[part], relay_recv.at[part])
        over_slots(lambda slot: start_rows(other_row, slot, part, relay_buf.at[part, slot]))

    own_columns = pl.ds(pl.multiple_of(row_id * tile_rows, tile_rows), tile_rows)

    def col_remote(part):
        return pltpu.make_async_remote_copy(
            src_ref=turned_ref.at[pl.ds(other_row * own + part * rows_in_part, rows_in_part)],
            dst_ref=col_buf.at[rows_of(part), own_columns, :],
            send_sem=col_send.at[part],
            recv_sem=col_recv.at[part],
            device_id=(other_row, col_id),
            device_id_type=MESH,
        )

    def own_col(part):
        return pltpu.make_async_copy(
            turned_ref.at[pl.ds(row_id * own + part * rows_in_part, rows_in_part)],
            col_buf.at[rows_of(part), own_columns, :],
            col_recv.at[part],
        )

    greet_all(row_count, col_count)

    ahead = min(2, parts)
    for part in range(ahead):
        relay_copy(part).start()
    for part in range(ahead):
        direct(part)
    for part in range(parts):
        col_remote(part).start()
        if part + ahead < parts:
            relay_copy(part + ahead).start()
        own_col(part).start()

    query_turned[...] = query_weight_ref[...].T
    value_turned[...] = value_weight_ref[...].T
    gate_turned[...] = gate_weight_ref[...].T
    chain_row = jnp.broadcast_to(chain_ref[...].astype(jnp.float32), (length, length))
    same_buf[...] = (chain_row.T == chain_row).astype(jnp.float32)
    penalty_row = mask_penalty * (1 - mask_ref[...]).astype(jnp.float32)
    penalty_buf[...] = jnp.broadcast_to(penalty_row, (length, length)).T

    for part in range(ahead):
        pass_on(part)
        if part + ahead < parts:
            direct(part + ahead)

    def bias_piece(part):
        return bias_buf.at[pair, side, row_id, part]

    def send_bias(part):
        def to_chip(step):
            other = lax.rem(chip + step, chip_total)
            pltpu.make_async_remote_copy(
                src_ref=bias_piece(part),
                dst_ref=bias_piece(part),
                send_sem=bias_send,
                recv_sem=bias_recv.at[part],
                device_id=(lax.rem(other, row_count), (other // row_count) * 2 + side),
                device_id_type=MESH,
            ).start()

        loop(1, chip_total, to_chip)

    def to_pair(part):
        return pltpu.make_async_remote_copy(
            src_ref=bias_buf.at[:, side, :, part],
            dst_ref=bias_buf.at[:, side, :, part],
            send_sem=pair_send.at[part],
            recv_sem=pair_recv.at[part],
            device_id=(row_id, col_id + 1 - 2 * side),
            device_id_type=MESH,
        )

    def hand_over(part):
        await_bytes(recv_buf.at[pl.ds(0, chip_total - 1), pl.ds(0, rows_in_part)], bias_recv.at[part])
        to_pair(part).start()

    def transition_row(position):
        sym_row = row_buf[position].astype(jnp.float32) + col_buf[position].astype(jnp.float32)
        first_norm = normalize(sym_row, gain_transition_ref[...]).astype(jnp.bfloat16)
        hidden_act = jax.nn.relu(
            jnp.dot(first_norm, hidden_weight_ref[...], preferred_element_type=jnp.float32)
        ).astype(jnp.bfloat16)
        carried = sym_row + jnp.dot(
            hidden_act, out_weight_ref[...], preferred_element_type=jnp.float32
        )
        carried_buf[position] = carried
        normed = normalize(carried, gain_attention_ref[...]).astype(jnp.bfloat16)
        normed_buf[position] = normed
        part = position // rows_in_part
        bias_buf[pair, side, row_id, part, position - part * rows_in_part] = lax.dot_general(
            bias_weight_ref[...],
            normed,
            (((1,), (1,)), ((), ())),
            preferred_element_type=jnp.float32,
        ).astype(jnp.bfloat16)

    def project_row(position):
        normed = normed_buf[position]
        normed_turned = normed.T

        def project(weight_ref):
            return jnp.dot(weight_ref[...], normed_turned, preferred_element_type=jnp.float32)

        key_buf[position] = jnp.dot(
            normed, key_weight_ref[...], preferred_element_type=jnp.float32
        ).astype(jnp.bfloat16)
        query_buf[position] = project(query_turned).astype(jnp.bfloat16)
        value_buf[position] = project(value_turned).astype(jnp.bfloat16)
        gate_buf[position] = jax.nn.sigmoid(project(gate_turned))

    def one_part(part):
        await_bytes(row_buf.at[rows_of(part)], row_recv.at[part])
        await_bytes(col_buf.at[rows_of(part)], col_recv.at[part])
        loop(part * rows_in_part, (part + 1) * rows_in_part, transition_row)
        send_bias(part)

        @pl.when(part + ahead < parts)
        def _():
            pass_on(part + ahead)

        loop(part * rows_in_part, (part + 1) * rows_in_part, project_row)

        @pl.when(part > 0)
        def _():
            hand_over(part - 1)

    loop(0, parts, one_part)
    hand_over(parts - 1)
    loop(0, parts, lambda part: await_bytes(bias_buf.at[:, side, :, part], pair_recv.at[part]))

    bias_rows = bias_buf.reshape(length * head_count, length)
    for lane, lanes in enumerate(lane_blocks):
        turned[lane] = bias_rows[:, lanes].astype(jnp.float32)
    for head in range(head_count):
        for lane, lanes in enumerate(lane_blocks):
            bias_full[head, :, lanes] = (
                turned[lane, pl.ds(head, length, stride=head_count), :]
                + chain_weight_ref[head] * same_buf[:, lanes]
                - penalty_buf[:, lanes]
            ) * LOG2_E

    strip = min(128, length)
    band = min(inner_total, max(128, head_dim))
    heads_in_band = band // head_dim
    head_of_lane = lax.broadcasted_iota(jnp.int32, (1, band), 1) // head_dim

    def attend_row(position):
        keys, queries, values = key_buf[position], query_buf[position], value_buf[position]

        def score(head):
            first = head // heads_in_band * band
            chosen = (head_of_lane == head % heads_in_band).astype(jnp.bfloat16)
            score_buf[head] = (
                jnp.dot(
                    keys[:, first : first + band] * chosen,
                    queries[first : first + band],
                    preferred_element_type=jnp.float32,
                )
                * score_scale
                + bias_full[head]
            )

        mixed = []
        for head in range(4):
            score(head)
        for head in range(head_count):
            if head + 4 < head_count:
                score(head + 4)
            rows = slice(head * head_dim, (head + 1) * head_dim)
            for start in range(0, length, strip):
                places = slice(start, start + strip)
                scores = score_buf[head, :, places]
                exponent = jnp.exp2(scores - jnp.max(scores, axis=0, keepdims=True))
                weight_buf[head, :, places] = (
                    exponent * (1.0 / jnp.sum(exponent, axis=0, keepdims=True))
                ).astype(jnp.bfloat16)
            mixture = jnp.dot(values[rows], weight_buf[head], preferred_element_type=jnp.float32)
            mixed.append((gate_buf[position, rows] * mixture).astype(jnp.bfloat16))
        gated = jnp.concatenate(mixed, axis=0).T
        update = jnp.dot(gated, output_weight_ref[...], preferred_element_type=jnp.float32)
        update = update.astype(jnp.bfloat16)
        update_buf[position] = update.reshape(device_total, own, channels)
        recv_buf[me, position] = update_buf[position, me]

        def to_peer(step):
            peer = lax.rem(me + step, device_total)
            pltpu.make_async_remote_copy(
                src_ref=update_buf.at[position, peer],
                dst_ref=recv_buf.at[me, position],
                send_sem=update_send,
                recv_sem=update_recv.at[position],
                device_id=(lax.rem(peer, row_count), peer // row_count),
                device_id_type=MESH,
            ).start()

        loop(1, device_total, to_peer)
        total = 2.0 * carried_buf[position] + update.astype(jnp.float32)
        for lane, lanes in enumerate(lane_blocks):
            turned[lane, pl.ds(position, length, stride=own), :] = total[:, lanes]

    loop(0, own, attend_row)

    my_columns = pl.ds(pl.multiple_of(row_id * own, own), own)
    totals = turned.reshape(len(lane_blocks), device_total, own, own, LANES)

    def summed(other, position, lane):
        devices = pl.ds(other * col_count, col_count)
        return (
            totals[lane, devices, position]
            + recv_buf[devices, position, :, lane_blocks[lane]].astype(jnp.float32)
        ).astype(jnp.bfloat16)

    def sum_remote(position):
        return pltpu.make_async_remote_copy(
            src_ref=sum_buf.at[:, position],
            dst_ref=out_ref.at[:, position, my_columns],
            send_sem=sum_send.at[position],
            recv_sem=sum_recv.at[position],
            device_id=(other_row, col_id),
            device_id_type=MESH,
        )

    def finish_position(position):
        await_bytes(recv_buf.at[pl.ds(0, device_total - 1), position], update_recv.at[position])
        for lane, lanes in enumerate(lane_blocks):
            sum_buf[:, position, :, lanes] = summed(other_row, position, lane)
        sum_remote(position).start()
        for lane, lanes in enumerate(lane_blocks):
            out_ref[:, position, my_columns, lanes] = summed(row_id, position, lane)

    loop(0, own, finish_position)

    await_bytes(recv_buf.at[pl.ds(0, device_total - 1)], update_send)
    await_bytes(
        recv_buf.at[pl.ds(0, chip_total - 1), pl.ds(0, own)], bias_send
    )

    await_bytes(row_buf.at[:, pl.ds(0, length - tile_cols)], row_send)

    def close_part(part):
        relay_copy(part).wait_send()
        col_remote(part).wait_send()
        to_pair(part).wait_send()

    loop(0, parts, close_part)

    def close_position(position):
        await_bytes(sum_buf.at[:, position], sum_recv.at[position])
        sum_remote(position).wait_send()

    loop(0, own, close_position)


def owned_columns(
    pair_state,
    residue_mask,
    chain_ids,
    gain_transition,
    hidden_weight,
    out_weight,
    gain_attention,
    query_weight,
    key_weight,
    value_weight,
    gate_weight,
    bias_weight,
    chain_weight,
    output_weight,
):
    tile_rows, tile_cols, channels = pair_state.shape
    row_count, col_count = lax.axis_size("row"), lax.axis_size("col")
    device_total = row_count * col_count
    head_count = chain_weight.shape[0]
    inner_total = key_weight.shape[1]
    length = tile_rows * row_count
    own = tile_cols // row_count
    span = col_count // row_count
    parts = PARTS
    rows_in_part = own // parts
    in_vmem = pl.BlockSpec(memory_space=pltpu.VMEM)
    in_smem = pl.BlockSpec(memory_space=pltpu.SMEM)
    dma = pltpu.SemaphoreType.DMA

    def half(*shape):
        return pltpu.VMEM(shape, jnp.bfloat16)

    def full(*shape):
        return pltpu.VMEM(shape, jnp.float32)

    out = pl.pallas_call(
        functools.partial(layer_kernel, row_count, col_count),
        out_shape=jax.ShapeDtypeStruct((col_count, own, tile_cols, channels), jnp.bfloat16),
        in_specs=[in_vmem] * 13 + [in_smem, in_vmem],
        out_specs=in_vmem,
        scratch_shapes=[
            half(own, length, channels),
            half(own, length, channels),
            half(parts, span, rows_in_part, tile_cols, channels),
            half(col_count // 2, 2, row_count, parts, rows_in_part, head_count, length),
            full(length, length),
            full(length, length),
            full(head_count, length, length),
            full(own, length, channels),
            half(own, length, channels),
            half(own, length, inner_total),
            half(own, inner_total, length),
            half(own, inner_total, length),
            full(own, inner_total, length),
            half(*query_weight.shape[::-1]),
            half(*value_weight.shape[::-1]),
            half(*gate_weight.shape[::-1]),
            full(head_count, length, length),
            half(head_count, length, length),
            half(own, device_total, own, channels),
            half(device_total, own, own, channels),
            full(channels // LANES, length * own, LANES),
            half(col_count, own, own, channels),
            dma((parts,)),
            dma((parts,)),
            dma,
            dma((parts,)),
            dma((parts,)),
            dma((parts,)),
            dma,
            dma((parts,)),
            dma((parts,)),
            dma((parts,)),
            dma,
            dma((own,)),
            dma((own,)),
            dma((own,)),
        ],
        compiler_params=pltpu.CompilerParams(
            collective_id=0, has_side_effects=True, vmem_limit_bytes=VMEM_LIMIT
        ),
        name="layer",
    )(
        pair_state.reshape(span, row_count, own, tile_cols, channels),
        jnp.transpose(pair_state, (1, 0, 2)),
        residue_mask[None, :],
        chain_ids[None, :],
        gain_transition[None, :],
        hidden_weight,
        out_weight,
        gain_attention[None, :],
        query_weight,
        key_weight,
        value_weight,
        gate_weight,
        bias_weight.T,
        chain_weight,
        output_weight,
    )
    return out.reshape(tile_rows, tile_cols, channels)


def per_device(pair_state, *others):
    tile_cols = pair_state.shape[1]
    row_count, col_count = lax.axis_size("row"), lax.axis_size("col")
    own = tile_cols // row_count
    length = row_count * pair_state.shape[0]
    fits = own == 8 and row_count == 2 and col_count % 2 == 0
    fits = fits and length == pair_state.shape[2] and length % LANES == 0
    if fits and others[11].shape[0] == own and pair_state.shape[0] == col_count * own:
        return owned_columns(pair_state, *others)
    return tile_layout(pair_state, *others)


def solution(mesh):
    placed = (
        P("row", "col", None),
        P(),
        P(),
        P(),
        P(),
        P(),
        P(),
        P(),
        P(),
        P(),
        P(),
        P(),
        P(),
        P(),
    )
    return jax.shard_map(
        per_device, mesh=mesh, in_specs=placed, out_specs=P("row", "col", None), check_vma=False
    )
```

```python
import functools
import math

import jax
import jax.numpy as jnp
from jax import lax
from jax.experimental import pallas as pl
from jax.experimental.pallas import tpu as pltpu
from jax.sharding import PartitionSpec as P

MESH = pl.DeviceIdType.MESH
VMEM_LIMIT = 60 * 1024 * 1024
LOG2_E = math.log2(math.e)
PARTS = 8
LANES = 128

mask_penalty = 1000000000.0
norm_epsilon = 1e-05


def normalize(values, gain):
    center = values - jnp.mean(values, axis=-1, keepdims=True)
    variance = jnp.mean(center * center, axis=-1, keepdims=True)
    return center * lax.rsqrt(variance + norm_epsilon) * gain


def mirror(tile):
    tile_rows, tile_cols, channels = tile.shape
    col_count = lax.axis_size("col")
    row_count = lax.axis_size("row")
    col_ratio = col_count // row_count
    piece_len = tile_cols * tile_cols // col_count
    sectioned = tile.reshape(col_ratio, col_count, piece_len, channels)
    sectioned = lax.all_to_all(sectioned, "col", split_axis=1, concat_axis=1, tiled=True)
    sectioned = sectioned.reshape(col_ratio, row_count, col_ratio, piece_len, channels)
    sectioned = lax.all_to_all(sectioned, "row", split_axis=1, concat_axis=1, tiled=True)
    sectioned = jnp.transpose(sectioned, (1, 0, 2, 3, 4)).reshape(
        col_count, col_ratio, piece_len, channels
    )
    sectioned = lax.all_to_all(sectioned, "col", split_axis=0, concat_axis=0, tiled=True)
    sectioned = jnp.transpose(sectioned, (1, 0, 2, 3)).reshape(
        col_ratio, tile_cols, tile_cols, channels
    )
    return jnp.transpose(sectioned, (0, 2, 1, 3)).reshape(tile_rows, tile_cols, channels)


def attend(query_part, gate_part, key_part, value_part, bias_part, head_count, output_weight):
    query_total = query_part.shape[0]
    key_total = key_part.shape[0]
    head_dim = query_part.shape[1] // head_count
    score_scale = 1.0 / math.sqrt(head_dim)
    query_heads = query_part.reshape(query_total, head_count, head_dim)
    key_heads = key_part.reshape(key_total, head_count, head_dim)
    value_heads = value_part.reshape(key_total, head_count, head_dim)
    scores = (
        jnp.einsum("jhd,khd->hjk", query_heads, key_heads, preferred_element_type=jnp.float32)
        * score_scale
        + bias_part
    )
    row_max = jnp.max(scores, axis=-1, keepdims=True)
    exponent = jnp.exp(scores - row_max)
    attn_weights = (exponent / jnp.sum(exponent, axis=-1, keepdims=True)).astype(jnp.bfloat16)
    mixture = jnp.einsum(
        "hjk,khd->jhd", attn_weights, value_heads, preferred_element_type=jnp.float32
    )
    gated = (gate_part * mixture.reshape(query_total, head_count * head_dim)).astype(jnp.bfloat16)
    return jnp.dot(gated, output_weight, preferred_element_type=jnp.float32).astype(jnp.bfloat16)


def mirror_layout(
    normed_tile,
    bias_tile,
    chain_ids,
    penalty,
    chain_weight,
    query_weight,
    key_weight,
    value_weight,
    gate_weight,
    output_weight,
):
    tile_rows, tile_cols, channels = normed_tile.shape
    head_count = bias_tile.shape[0]
    row_start = lax.axis_index("row") * tile_rows
    flat_tile = normed_tile.reshape(tile_rows * tile_cols, channels)
    key_tile = (
        jnp.dot(flat_tile, key_weight, preferred_element_type=jnp.float32)
        .astype(jnp.bfloat16)
        .reshape(tile_rows, tile_cols, -1)
    )
    value_tile = (
        jnp.dot(flat_tile, value_weight, preferred_element_type=jnp.float32)
        .astype(jnp.bfloat16)
        .reshape(tile_rows, tile_cols, -1)
    )
    key_all, value_all = (
        lax.all_gather(key_tile, "row", axis=0, tiled=True),
        lax.all_gather(value_tile, "row", axis=0, tiled=True),
    )
    bias_rows = lax.all_gather(bias_tile, "col", axis=2, tiled=True)
    chain_rows = lax.dynamic_slice_in_dim(chain_ids, row_start, tile_rows, 0)
    same_chain = (chain_rows[:, None] == chain_ids[None, :]).astype(jnp.float32)
    bias_full = (
        bias_rows.astype(jnp.float32)
        + chain_weight[:, None, None] * same_chain[None]
        - penalty[None, None, :]
    )
    query_tile = (
        jnp.dot(flat_tile, query_weight, preferred_element_type=jnp.float32)
        .astype(jnp.bfloat16)
        .reshape(tile_rows, tile_cols, -1)
    )
    gate_tile = jax.nn.sigmoid(
        jnp.dot(flat_tile, gate_weight, preferred_element_type=jnp.float32)
    ).reshape(tile_rows, tile_cols, -1)

    def one_column(position):
        query_part = lax.dynamic_index_in_dim(query_tile, position, 1, keepdims=False)
        gate_part = lax.dynamic_index_in_dim(gate_tile, position, 1, keepdims=False)
        key_part = lax.dynamic_index_in_dim(key_all, position, 1, keepdims=False)
        value_part = lax.dynamic_index_in_dim(value_all, position, 1, keepdims=False)
        return attend(
            query_part, gate_part, key_part, value_part, bias_full, head_count, output_weight
        )

    results = lax.map(one_column, jnp.arange(tile_cols, dtype=jnp.int32))
    return jnp.transpose(results, (1, 0, 2))


def tile_layout(
    pair_state,
    residue_mask,
    chain_ids,
    gain_transition,
    hidden_weight,
    out_weight,
    gain_attention,
    query_weight,
    key_weight,
    value_weight,
    gate_weight,
    bias_weight,
    chain_weight,
    output_weight,
):
    tile_rows, tile_cols, channels = pair_state.shape
    head_count = chain_weight.shape[0]
    mirrored = mirror(pair_state)
    sym_tile = pair_state.astype(jnp.float32) + mirrored.astype(jnp.float32)
    flat_sym = sym_tile.reshape(tile_rows * tile_cols, channels)
    first_norm = normalize(flat_sym, gain_transition).astype(jnp.bfloat16)
    hidden_act = jax.nn.relu(
        jnp.dot(first_norm, hidden_weight, preferred_element_type=jnp.float32)
    ).astype(jnp.bfloat16)
    carried = flat_sym + jnp.dot(hidden_act, out_weight, preferred_element_type=jnp.float32)
    normed = normalize(carried, gain_attention).astype(jnp.bfloat16)
    bias_tile = (
        jnp.einsum("pd,dh->hp", normed, bias_weight, preferred_element_type=jnp.float32)
        .astype(jnp.bfloat16)
        .reshape(head_count, tile_rows, tile_cols)
    )
    penalty = mask_penalty * (1 - residue_mask).astype(jnp.float32)
    normed_tile = normed.reshape(tile_rows, tile_cols, channels)
    arguments = (
        normed_tile,
        bias_tile,
        chain_ids,
        penalty,
        chain_weight,
        query_weight,
        key_weight,
        value_weight,
        gate_weight,
        output_weight,
    )
    own_update = mirror_layout(*arguments)
    other_update = mirror(own_update)
    total = (
        2.0 * carried.reshape(tile_rows, tile_cols, channels)
        + own_update.astype(jnp.float32)
        + other_update.astype(jnp.float32)
    )
    return total.astype(jnp.bfloat16)


def greet_all(row_count, col_count):
    device_total = row_count * col_count
    me = lax.axis_index("col") * row_count + lax.axis_index("row")
    barrier = pltpu.get_barrier_semaphore()

    def greet(step, carry):
        peer = lax.rem(me + step, device_total)
        pl.semaphore_signal(
            barrier,
            inc=1,
            device_id=(lax.rem(peer, row_count), peer // row_count),
            device_id_type=MESH,
        )
        return carry

    lax.fori_loop(1, device_total, greet, 0)
    pl.semaphore_wait(barrier, device_total - 1)


def layer_kernel(
    row_count,
    col_count,
    tile_ref,
    mask_ref,
    chain_ref,
    gain_transition_ref,
    hidden_weight_hbm,
    out_weight_hbm,
    gain_attention_ref,
    query_weight_hbm,
    key_weight_hbm,
    value_weight_hbm,
    gate_weight_hbm,
    bias_weight_ref,
    chain_weight_ref,
    output_weight_hbm,
    out_ref,
    tile_buf,
    hidden_weight_ref,
    out_weight_ref,
    query_weight_ref,
    key_weight_ref,
    value_weight_ref,
    gate_weight_ref,
    output_weight_ref,
    row_buf,
    col_buf,
    turned_ref,
    relay_buf,
    bias_buf,
    same_buf,
    penalty_buf,
    bias_full,
    carried_buf,
    normed_buf,
    key_buf,
    query_buf,
    value_buf,
    gate_buf,
    query_turned,
    value_turned,
    gate_turned,
    score_buf,
    weight_buf,
    update_buf,
    recv_buf,
    turned,
    sum_buf,
    load_done,
    relay_send,
    relay_recv,
    row_send,
    row_recv,
    col_send,
    col_recv,
    quad_send,
    quad_recv,
    fan_send,
    fan_recv,
    last_send,
    last_recv,
    pair_send,
    pair_recv,
    update_send,
    update_recv,
    sum_send,
    sum_recv,
):
    span, _, own, tile_cols, channels = tile_ref.shape
    parts, _, rows_in_part = relay_buf.shape[:3]
    length = row_buf.shape[1]
    tile_rows = length // row_count
    head_count = bias_weight_ref.shape[0]
    inner_total = key_weight_ref.shape[1]
    head_dim = inner_total // head_count
    score_scale = LOG2_E / math.sqrt(head_dim)
    device_total = row_count * col_count
    chip_total = device_total // 2
    row_id, col_id = lax.axis_index("row"), lax.axis_index("col")
    other_row = 1 - row_id
    me = col_id * row_count + row_id
    side = lax.rem(col_id, 2)
    pair = col_id // 2
    chip = pair * row_count + row_id
    quarters = col_count // 4
    far, quarter = pair // quarters, lax.rem(pair, quarters)
    opposite_col = lax.rem(col_id + span, col_count)
    last = parts - 1
    lane_blocks = [slice(start, start + LANES) for start in range(0, channels, LANES)]

    def loop(first, last, body):
        def one(step, carry):
            body(step)
            return carry

        lax.fori_loop(first, last, one, 0)

    def await_bytes(like, semaphore):
        pltpu.make_async_copy(like, like, semaphore).wait()

    def rows_of(part):
        return pl.ds(part * rows_in_part, rows_in_part)

    def relay_copy(part):
        return pltpu.make_async_remote_copy(
            src_ref=tile_ref.at[:, other_row, rows_of(part)],
            dst_ref=relay_buf.at[part],
            send_sem=relay_send.at[part],
            recv_sem=relay_recv.at[part],
            device_id=(other_row, col_id),
            device_id_type=MESH,
        )

    def start_rows(origin, slot, part, source):
        target = origin * span + slot
        columns = pl.ds(pl.multiple_of(col_id * tile_cols, tile_cols), tile_cols)
        landing = row_buf.at[rows_of(part), columns, :]

        @pl.when(target != col_id)
        def _():
            pltpu.make_async_remote_copy(
                src_ref=source,
                dst_ref=landing,
                send_sem=row_send,
                recv_sem=row_recv.at[part],
                device_id=(row_id, target),
                device_id_type=MESH,
            ).start()

        @pl.when(target == col_id)
        def _():
            pltpu.make_async_copy(source, landing, row_recv.at[part]).start()

    def over_slots(body):
        loop(0, span, lambda step: body(lax.rem(col_id + step, span)))

    def direct(part):
        over_slots(
            lambda slot: start_rows(row_id, slot, part, tile_ref.at[slot, row_id, rows_of(part)])
        )

    def pass_on(part):
        await_bytes(relay_buf.at[part], relay_recv.at[part])
        over_slots(lambda slot: start_rows(other_row, slot, part, relay_buf.at[part, slot]))

    own_columns = pl.ds(pl.multiple_of(row_id * tile_rows, tile_rows), tile_rows)

    def col_remote(part):
        return pltpu.make_async_remote_copy(
            src_ref=turned_ref.at[rows_of(part)],
            dst_ref=col_buf.at[rows_of(part), own_columns, :],
            send_sem=col_send.at[part],
            recv_sem=col_recv.at[part],
            device_id=(other_row, col_id),
            device_id_type=MESH,
        )

    loads = [
        pltpu.make_async_copy(source, target, load_done.at[index])
        for index, (source, target) in enumerate(
            (
                (tile_ref, tile_buf),
                (hidden_weight_hbm, hidden_weight_ref),
                (out_weight_hbm, out_weight_ref),
                (query_weight_hbm, query_weight_ref),
                (key_weight_hbm, key_weight_ref),
                (value_weight_hbm, value_weight_ref),
                (gate_weight_hbm, gate_weight_ref),
                (output_weight_hbm, output_weight_ref),
            )
        )
    ]
    loads[0].start()
    greet_all(row_count, col_count)

    ahead = min(2, parts)
    for part in range(parts):
        relay_copy(part).start()
    for part in range(ahead):
        direct(part)
    loads[0].wait()
    for load in loads[1:]:
        load.start()
    tile_flat = tile_buf.reshape(tile_rows * tile_cols, channels)
    for lane, lanes in enumerate(lane_blocks):
        turned[lane] = tile_flat[:, lanes].astype(jnp.float32)

    def turned_column(column, lane):
        return turned[lane, pl.ds(column, tile_rows, stride=tile_cols), :].astype(jnp.bfloat16)

    for position in range(own):
        for lane, lanes in enumerate(lane_blocks):
            turned_ref[position, :, lanes] = turned_column(other_row * own + position, lane)
    for part in range(parts):
        col_remote(part).start()
    for position in range(own):
        for lane, lanes in enumerate(lane_blocks):
            col_buf[position, own_columns, lanes] = turned_column(row_id * own + position, lane)
    for load in loads[1:]:
        load.wait()
    query_turned[...] = query_weight_ref[...].T
    value_turned[...] = value_weight_ref[...].T
    gate_turned[...] = gate_weight_ref[...].T
    chain_row = jnp.broadcast_to(chain_ref[...].astype(jnp.float32), (length, length))
    same_buf[...] = (chain_row.T == chain_row).astype(jnp.float32)
    penalty_row = mask_penalty * (1 - mask_ref[...]).astype(jnp.float32)
    penalty_buf[...] = jnp.broadcast_to(penalty_row, (length, length)).T

    for part in range(parts):
        pass_on(part)
        if part + ahead < parts:
            direct(part + ahead)

    def bias_piece(part):
        return bias_buf.at[far, quarter, side, row_id, part]

    def quad_copy(part, device):
        return pltpu.make_async_remote_copy(
            src_ref=bias_piece(part),
            dst_ref=bias_piece(part),
            send_sem=quad_send,
            recv_sem=quad_recv.at[part],
            device_id=device,
            device_id_type=MESH,
        )

    def send_quad(part):
        quad_copy(part, (row_id, opposite_col)).start()
        quad_copy(part, (other_row, opposite_col)).start()
        quad_copy(part, (other_row, col_id)).start()

    def pieces(count, rows):
        return recv_buf.at[pl.ds(0, count), pl.ds(0, rows)]

    def send_fan(part):
        await_bytes(pieces(3, rows_in_part), quad_recv.at[part])

        def to_quarter(step):
            target = lax.rem(quarter + step, quarters)
            pltpu.make_async_remote_copy(
                src_ref=bias_buf.at[:, quarter, side, :, part],
                dst_ref=bias_buf.at[:, quarter, side, :, part],
                send_sem=fan_send,
                recv_sem=fan_recv.at[part],
                device_id=(row_id, (far * quarters + target) * 2 + side),
                device_id_type=MESH,
            ).start()

        loop(1, quarters, to_quarter)

    def send_last():
        def to_chip(step):
            other = lax.rem(chip + step, chip_total)
            pltpu.make_async_remote_copy(
                src_ref=bias_piece(last),
                dst_ref=bias_piece(last),
                send_sem=last_send,
                recv_sem=last_recv,
                device_id=(lax.rem(other, row_count), (other // row_count) * 2 + side),
                device_id_type=MESH,
            ).start()

        loop(1, chip_total, to_chip)

    def to_pair(part):
        return pltpu.make_async_remote_copy(
            src_ref=bias_buf.at[:, :, side, :, part],
            dst_ref=bias_buf.at[:, :, side, :, part],
            send_sem=pair_send.at[part],
            recv_sem=pair_recv.at[part],
            device_id=(row_id, col_id + 1 - 2 * side),
            device_id_type=MESH,
        )

    def hand_over(part):
        await_bytes(pieces(4 * (quarters - 1), rows_in_part), fan_recv.at[part])
        to_pair(part).start()

    def transition_row(position):
        sym_row = row_buf[position].astype(jnp.float32) + col_buf[position].astype(jnp.float32)
        first_norm = normalize(sym_row, gain_transition_ref[...]).astype(jnp.bfloat16)
        hidden_act = jax.nn.relu(
            jnp.dot(first_norm, hidden_weight_ref[...], preferred_element_type=jnp.float32)
        ).astype(jnp.bfloat16)
        carried = sym_row + jnp.dot(
            hidden_act, out_weight_ref[...], preferred_element_type=jnp.float32
        )
        carried_buf[position] = carried
        normed = normalize(carried, gain_attention_ref[...]).astype(jnp.bfloat16)
        normed_buf[position] = normed
        part = position // rows_in_part
        bias_buf[far, quarter, side, row_id, part, position - part * rows_in_part] = lax.dot_general(
            bias_weight_ref[...],
            normed,
            (((1,), (1,)), ((), ())),
            preferred_element_type=jnp.float32,
        ).astype(jnp.bfloat16)

    def project_row(position):
        normed = normed_buf[position]
        normed_turned = normed.T

        def project(weight_ref):
            return jnp.dot(weight_ref[...], normed_turned, preferred_element_type=jnp.float32)

        key_buf[position] = jnp.dot(
            normed, key_weight_ref[...], preferred_element_type=jnp.float32
        ).astype(jnp.bfloat16)
        query_buf[position] = project(query_turned).astype(jnp.bfloat16)
        value_buf[position] = project(value_turned).astype(jnp.bfloat16)
        gate_buf[position] = jax.nn.sigmoid(project(gate_turned))

    def await_part(part):
        await_bytes(row_buf.at[rows_of(part)], row_recv.at[part])
        await_bytes(turned_ref.at[rows_of(part)], col_recv.at[part])

    def one_part(part):
        await_part(part)
        loop(part * rows_in_part, (part + 1) * rows_in_part, transition_row)
        send_quad(part)

    loop(0, last, one_part)
    await_part(last)
    loop(0, last - 1, send_fan)
    loop(last * rows_in_part, own, transition_row)
    send_last()
    send_fan(last - 1)
    loop(0, own // 2, project_row)
    loop(0, last - 1, hand_over)
    loop(own // 2, own, project_row)
    hand_over(last - 1)
    await_bytes(pieces(chip_total - 1, rows_in_part), last_recv)
    to_pair(last).start()
    loop(0, parts, lambda part: await_bytes(bias_buf.at[:, :, side, :, part], pair_recv.at[part]))

    bias_rows = bias_buf.reshape(length * head_count, length)
    for lane, lanes in enumerate(lane_blocks):
        turned[lane] = bias_rows[:, lanes].astype(jnp.float32)
    for head in range(head_count):
        for lane, lanes in enumerate(lane_blocks):
            bias_full[head, :, lanes] = (
                turned[lane, pl.ds(head, length, stride=head_count), :]
                + chain_weight_ref[head] * same_buf[:, lanes]
                - penalty_buf[:, lanes]
            ) * LOG2_E

    strip = min(128, length)
    band = min(inner_total, max(128, head_dim))
    heads_in_band = band // head_dim
    head_of_lane = lax.broadcasted_iota(jnp.int32, (1, band), 1) // head_dim

    def attend_row(position):
        keys, queries, values = key_buf[position], query_buf[position], value_buf[position]

        def score(head):
            first = head // heads_in_band * band
            chosen = (head_of_lane == head % heads_in_band).astype(jnp.bfloat16)
            score_buf[head] = (
                jnp.dot(
                    keys[:, first : first + band] * chosen,
                    queries[first : first + band],
                    preferred_element_type=jnp.float32,
                )
                * score_scale
                + bias_full[head]
            )

        mixed = []
        for head in range(4):
            score(head)
        for head in range(head_count):
            if head + 4 < head_count:
                score(head + 4)
            rows = slice(head * head_dim, (head + 1) * head_dim)
            for start in range(0, length, strip):
                places = slice(start, start + strip)
                scores = score_buf[head, :, places]
                exponent = jnp.exp2(scores - jnp.max(scores, axis=0, keepdims=True))
                weight_buf[head, :, places] = (
                    exponent * (1.0 / jnp.sum(exponent, axis=0, keepdims=True))
                ).astype(jnp.bfloat16)
            mixture = jnp.dot(values[rows], weight_buf[head], preferred_element_type=jnp.float32)
            mixed.append((gate_buf[position, rows] * mixture).astype(jnp.bfloat16))
        gated = jnp.concatenate(mixed, axis=0).T
        update = jnp.dot(gated, output_weight_ref[...], preferred_element_type=jnp.float32)
        update = update.astype(jnp.bfloat16)
        update_buf[position] = update.reshape(device_total, own, channels)
        recv_buf[me, position] = update_buf[position, me]

        def to_peer(step):
            peer = lax.rem(me + step, device_total)
            pltpu.make_async_remote_copy(
                src_ref=update_buf.at[position, peer],
                dst_ref=recv_buf.at[me, position],
                send_sem=update_send,
                recv_sem=update_recv.at[position],
                device_id=(lax.rem(peer, row_count), peer // row_count),
                device_id_type=MESH,
            ).start()

        loop(1, device_total, to_peer)
        total = 2.0 * carried_buf[position] + update.astype(jnp.float32)
        for lane, lanes in enumerate(lane_blocks):
            turned[lane, pl.ds(position, length, stride=own), :] = total[:, lanes]

    loop(0, own, attend_row)

    my_columns = pl.ds(pl.multiple_of(row_id * own, own), own)
    totals = turned.reshape(len(lane_blocks), device_total, own, own, LANES)

    def summed(other, position, lane):
        devices = pl.ds(other * col_count, col_count)
        return (
            totals[lane, devices, position]
            + recv_buf[devices, position, :, lane_blocks[lane]].astype(jnp.float32)
        ).astype(jnp.bfloat16)

    def sum_remote(position):
        return pltpu.make_async_remote_copy(
            src_ref=sum_buf.at[:, position],
            dst_ref=out_ref.at[:, position, my_columns],
            send_sem=sum_send.at[position],
            recv_sem=sum_recv.at[position],
            device_id=(other_row, col_id),
            device_id_type=MESH,
        )

    def finish_position(position):
        await_bytes(recv_buf.at[pl.ds(0, device_total - 1), position], update_recv.at[position])
        for lane, lanes in enumerate(lane_blocks):
            sum_buf[:, position, :, lanes] = summed(other_row, position, lane)
        sum_remote(position).start()
        for lane, lanes in enumerate(lane_blocks):
            out_ref[:, position, my_columns, lanes] = summed(row_id, position, lane)

    loop(0, own, finish_position)

    await_bytes(recv_buf.at[pl.ds(0, device_total - 1)], update_send)
    await_bytes(pieces(3, last * rows_in_part), quad_send)
    await_bytes(pieces(4 * (quarters - 1), last * rows_in_part), fan_send)
    await_bytes(pieces(chip_total - 1, rows_in_part), last_send)
    await_bytes(row_buf.at[:, pl.ds(0, length - tile_cols)], row_send)

    def close_part(part):
        relay_copy(part).wait_send()
        col_remote(part).wait_send()
        to_pair(part).wait_send()

    loop(0, parts, close_part)

    def close_position(position):
        await_bytes(sum_buf.at[:, position], sum_recv.at[position])
        sum_remote(position).wait_send()

    loop(0, own, close_position)


def owned_columns(
    pair_state,
    residue_mask,
    chain_ids,
    gain_transition,
    hidden_weight,
    out_weight,
    gain_attention,
    query_weight,
    key_weight,
    value_weight,
    gate_weight,
    bias_weight,
    chain_weight,
    output_weight,
):
    tile_rows, tile_cols, channels = pair_state.shape
    row_count, col_count = lax.axis_size("row"), lax.axis_size("col")
    device_total = row_count * col_count
    head_count = chain_weight.shape[0]
    inner_total = key_weight.shape[1]
    length = tile_rows * row_count
    own = tile_cols // row_count
    span = col_count // row_count
    parts = PARTS
    rows_in_part = own // parts
    in_vmem = pl.BlockSpec(memory_space=pltpu.VMEM)
    in_hbm = pl.BlockSpec(memory_space=pl.ANY)
    in_smem = pl.BlockSpec(memory_space=pltpu.SMEM)
    dma = pltpu.SemaphoreType.DMA

    def half(*shape):
        return pltpu.VMEM(shape, jnp.bfloat16)

    def full(*shape):
        return pltpu.VMEM(shape, jnp.float32)

    out = pl.pallas_call(
        functools.partial(layer_kernel, row_count, col_count),
        out_shape=jax.ShapeDtypeStruct((col_count, own, tile_cols, channels), jnp.bfloat16),
        in_specs=[
            in_hbm,
            in_vmem,
            in_vmem,
            in_vmem,
            in_hbm,
            in_hbm,
            in_vmem,
            in_hbm,
            in_hbm,
            in_hbm,
            in_hbm,
            in_vmem,
            in_smem,
            in_hbm,
        ],
        out_specs=in_vmem,
        scratch_shapes=[
            half(span, row_count, own, tile_cols, channels),
            half(*hidden_weight.shape),
            half(*out_weight.shape),
            half(*query_weight.shape),
            half(*key_weight.shape),
            half(*value_weight.shape),
            half(*gate_weight.shape),
            half(*output_weight.shape),
            half(own, length, channels),
            half(own, length, channels),
            half(own, tile_rows, channels),
            half(parts, span, rows_in_part, tile_cols, channels),
            half(2, col_count // 4, 2, row_count, parts, rows_in_part, head_count, length),
            full(length, length),
            full(length, length),
            full(head_count, length, length),
            full(own, length, channels),
            half(own, length, channels),
            half(own, length, inner_total),
            half(own, inner_total, length),
            half(own, inner_total, length),
            full(own, inner_total, length),
            half(*query_weight.shape[::-1]),
            half(*value_weight.shape[::-1]),
            half(*gate_weight.shape[::-1]),
            full(head_count, length, length),
            half(head_count, length, length),
            half(own, device_total, own, channels),
            half(device_total, own, own, channels),
            full(channels // LANES, length * own, LANES),
            half(col_count, own, own, channels),
            dma((8,)),
            dma((parts,)),
            dma((parts,)),
            dma,
            dma((parts,)),
            dma((parts,)),
            dma((parts,)),
            dma,
            dma((parts,)),
            dma,
            dma((parts,)),
            dma,
            dma,
            dma((parts,)),
            dma((parts,)),
            dma,
            dma((own,)),
            dma((own,)),
            dma((own,)),
        ],
        compiler_params=pltpu.CompilerParams(
            collective_id=0, has_side_effects=True, vmem_limit_bytes=VMEM_LIMIT
        ),
        name="layer",
    )(
        pair_state.reshape(span, row_count, own, tile_cols, channels),
        residue_mask[None, :],
        chain_ids[None, :],
        gain_transition[None, :],
        hidden_weight,
        out_weight,
        gain_attention[None, :],
        query_weight,
        key_weight,
        value_weight,
        gate_weight,
        bias_weight.T,
        chain_weight,
        output_weight,
    )
    return out.reshape(tile_rows, tile_cols, channels)


def per_device(pair_state, *others):
    tile_cols = pair_state.shape[1]
    row_count, col_count = lax.axis_size("row"), lax.axis_size("col")
    own = tile_cols // row_count
    length = row_count * pair_state.shape[0]
    fits = own == 8 and row_count == 2 and col_count % 4 == 0
    fits = fits and length == pair_state.shape[2] and length % LANES == 0
    if fits and others[11].shape[0] == own and pair_state.shape[0] == col_count * own:
        return owned_columns(pair_state, *others)
    return tile_layout(pair_state, *others)


def solution(mesh):
    placed = (
        P("row", "col", None),
        P(),
        P(),
        P(),
        P(),
        P(),
        P(),
        P(),
        P(),
        P(),
        P(),
        P(),
        P(),
        P(),
    )
    return jax.shard_map(
        per_device, mesh=mesh, in_specs=placed, out_specs=P("row", "col", None), check_vma=False
    )
```

```python
import functools
import math

import jax
import jax.numpy as jnp
from jax import lax
from jax.experimental import pallas as pl
from jax.experimental.pallas import tpu as pltpu
from jax.sharding import PartitionSpec as P

MESH = pl.DeviceIdType.MESH
VMEM_LIMIT = 60 * 1024 * 1024
LOG2_E = math.log2(math.e)
PARTS = 8
LANES = 128

mask_penalty = 1000000000.0
norm_epsilon = 1e-05


def normalize(values, gain):
    center = values - jnp.mean(values, axis=-1, keepdims=True)
    variance = jnp.mean(center * center, axis=-1, keepdims=True)
    return center * lax.rsqrt(variance + norm_epsilon) * gain


def mirror(tile):
    tile_rows, tile_cols, channels = tile.shape
    col_count = lax.axis_size("col")
    row_count = lax.axis_size("row")
    col_ratio = col_count // row_count
    piece_len = tile_cols * tile_cols // col_count
    sectioned = tile.reshape(col_ratio, col_count, piece_len, channels)
    sectioned = lax.all_to_all(sectioned, "col", split_axis=1, concat_axis=1, tiled=True)
    sectioned = sectioned.reshape(col_ratio, row_count, col_ratio, piece_len, channels)
    sectioned = lax.all_to_all(sectioned, "row", split_axis=1, concat_axis=1, tiled=True)
    sectioned = jnp.transpose(sectioned, (1, 0, 2, 3, 4)).reshape(
        col_count, col_ratio, piece_len, channels
    )
    sectioned = lax.all_to_all(sectioned, "col", split_axis=0, concat_axis=0, tiled=True)
    sectioned = jnp.transpose(sectioned, (1, 0, 2, 3)).reshape(
        col_ratio, tile_cols, tile_cols, channels
    )
    return jnp.transpose(sectioned, (0, 2, 1, 3)).reshape(tile_rows, tile_cols, channels)


def attend(query_part, gate_part, key_part, value_part, bias_part, head_count, output_weight):
    query_total = query_part.shape[0]
    key_total = key_part.shape[0]
    head_dim = query_part.shape[1] // head_count
    score_scale = 1.0 / math.sqrt(head_dim)
    query_heads = query_part.reshape(query_total, head_count, head_dim)
    key_heads = key_part.reshape(key_total, head_count, head_dim)
    value_heads = value_part.reshape(key_total, head_count, head_dim)
    scores = (
        jnp.einsum("jhd,khd->hjk", query_heads, key_heads, preferred_element_type=jnp.float32)
        * score_scale
        + bias_part
    )
    row_max = jnp.max(scores, axis=-1, keepdims=True)
    exponent = jnp.exp(scores - row_max)
    attn_weights = (exponent / jnp.sum(exponent, axis=-1, keepdims=True)).astype(jnp.bfloat16)
    mixture = jnp.einsum(
        "hjk,khd->jhd", attn_weights, value_heads, preferred_element_type=jnp.float32
    )
    gated = (gate_part * mixture.reshape(query_total, head_count * head_dim)).astype(jnp.bfloat16)
    return jnp.dot(gated, output_weight, preferred_element_type=jnp.float32).astype(jnp.bfloat16)


def mirror_layout(
    normed_tile,
    bias_tile,
    chain_ids,
    penalty,
    chain_weight,
    query_weight,
    key_weight,
    value_weight,
    gate_weight,
    output_weight,
):
    tile_rows, tile_cols, channels = normed_tile.shape
    head_count = bias_tile.shape[0]
    row_start = lax.axis_index("row") * tile_rows
    flat_tile = normed_tile.reshape(tile_rows * tile_cols, channels)
    key_tile = (
        jnp.dot(flat_tile, key_weight, preferred_element_type=jnp.float32)
        .astype(jnp.bfloat16)
        .reshape(tile_rows, tile_cols, -1)
    )
    value_tile = (
        jnp.dot(flat_tile, value_weight, preferred_element_type=jnp.float32)
        .astype(jnp.bfloat16)
        .reshape(tile_rows, tile_cols, -1)
    )
    key_all, value_all = (
        lax.all_gather(key_tile, "row", axis=0, tiled=True),
        lax.all_gather(value_tile, "row", axis=0, tiled=True),
    )
    bias_rows = lax.all_gather(bias_tile, "col", axis=2, tiled=True)
    chain_rows = lax.dynamic_slice_in_dim(chain_ids, row_start, tile_rows, 0)
    same_chain = (chain_rows[:, None] == chain_ids[None, :]).astype(jnp.float32)
    bias_full = (
        bias_rows.astype(jnp.float32)
        + chain_weight[:, None, None] * same_chain[None]
        - penalty[None, None, :]
    )
    query_tile = (
        jnp.dot(flat_tile, query_weight, preferred_element_type=jnp.float32)
        .astype(jnp.bfloat16)
        .reshape(tile_rows, tile_cols, -1)
    )
    gate_tile = jax.nn.sigmoid(
        jnp.dot(flat_tile, gate_weight, preferred_element_type=jnp.float32)
    ).reshape(tile_rows, tile_cols, -1)

    def one_column(position):
        query_part = lax.dynamic_index_in_dim(query_tile, position, 1, keepdims=False)
        gate_part = lax.dynamic_index_in_dim(gate_tile, position, 1, keepdims=False)
        key_part = lax.dynamic_index_in_dim(key_all, position, 1, keepdims=False)
        value_part = lax.dynamic_index_in_dim(value_all, position, 1, keepdims=False)
        return attend(
            query_part, gate_part, key_part, value_part, bias_full, head_count, output_weight
        )

    results = lax.map(one_column, jnp.arange(tile_cols, dtype=jnp.int32))
    return jnp.transpose(results, (1, 0, 2))


def tile_layout(
    pair_state,
    residue_mask,
    chain_ids,
    gain_transition,
    hidden_weight,
    out_weight,
    gain_attention,
    query_weight,
    key_weight,
    value_weight,
    gate_weight,
    bias_weight,
    chain_weight,
    output_weight,
):
    tile_rows, tile_cols, channels = pair_state.shape
    head_count = chain_weight.shape[0]
    mirrored = mirror(pair_state)
    sym_tile = pair_state.astype(jnp.float32) + mirrored.astype(jnp.float32)
    flat_sym = sym_tile.reshape(tile_rows * tile_cols, channels)
    first_norm = normalize(flat_sym, gain_transition).astype(jnp.bfloat16)
    hidden_act = jax.nn.relu(
        jnp.dot(first_norm, hidden_weight, preferred_element_type=jnp.float32)
    ).astype(jnp.bfloat16)
    carried = flat_sym + jnp.dot(hidden_act, out_weight, preferred_element_type=jnp.float32)
    normed = normalize(carried, gain_attention).astype(jnp.bfloat16)
    bias_tile = (
        jnp.einsum("pd,dh->hp", normed, bias_weight, preferred_element_type=jnp.float32)
        .astype(jnp.bfloat16)
        .reshape(head_count, tile_rows, tile_cols)
    )
    penalty = mask_penalty * (1 - residue_mask).astype(jnp.float32)
    normed_tile = normed.reshape(tile_rows, tile_cols, channels)
    arguments = (
        normed_tile,
        bias_tile,
        chain_ids,
        penalty,
        chain_weight,
        query_weight,
        key_weight,
        value_weight,
        gate_weight,
        output_weight,
    )
    own_update = mirror_layout(*arguments)
    other_update = mirror(own_update)
    total = (
        2.0 * carried.reshape(tile_rows, tile_cols, channels)
        + own_update.astype(jnp.float32)
        + other_update.astype(jnp.float32)
    )
    return total.astype(jnp.bfloat16)


def greet_all(row_count, col_count):
    device_total = row_count * col_count
    me = lax.axis_index("col") * row_count + lax.axis_index("row")
    barrier = pltpu.get_barrier_semaphore()

    def greet(step, carry):
        peer = lax.rem(me + step, device_total)
        pl.semaphore_signal(
            barrier,
            inc=1,
            device_id=(lax.rem(peer, row_count), peer // row_count),
            device_id_type=MESH,
        )
        return carry

    lax.fori_loop(1, device_total, greet, 0)
    pl.semaphore_wait(barrier, device_total - 1)


def layer_kernel(
    row_count,
    col_count,
    tile_ref,
    mask_ref,
    chain_ref,
    gain_transition_ref,
    hidden_weight_hbm,
    out_weight_hbm,
    gain_attention_ref,
    query_weight_hbm,
    key_weight_hbm,
    value_weight_hbm,
    gate_weight_hbm,
    bias_weight_ref,
    chain_weight_ref,
    output_weight_hbm,
    out_ref,
    tile_buf,
    hidden_weight_ref,
    out_weight_ref,
    query_weight_ref,
    key_weight_ref,
    value_weight_ref,
    gate_weight_ref,
    output_weight_ref,
    row_buf,
    col_buf,
    turned_ref,
    relay_buf,
    bias_buf,
    same_buf,
    penalty_buf,
    bias_full,
    carried_buf,
    normed_buf,
    key_buf,
    query_buf,
    value_buf,
    gate_buf,
    query_turned,
    value_turned,
    gate_turned,
    score_buf,
    weight_buf,
    update_buf,
    recv_buf,
    turned,
    sum_buf,
    load_done,
    relay_send,
    relay_recv,
    row_send,
    row_recv,
    col_send,
    col_recv,
    quad_send,
    quad_recv,
    fan_send,
    fan_recv,
    last_send,
    last_recv,
    pair_send,
    pair_recv,
    update_send,
    update_recv,
    sum_send,
    sum_recv,
):
    span, _, own, tile_cols, channels = tile_ref.shape
    parts, _, rows_in_part = relay_buf.shape[:3]
    length = row_buf.shape[1]
    tile_rows = length // row_count
    head_count = bias_weight_ref.shape[0]
    inner_total = key_weight_ref.shape[1]
    head_dim = inner_total // head_count
    score_scale = LOG2_E / math.sqrt(head_dim)
    device_total = row_count * col_count
    chip_total = device_total // 2
    row_id, col_id = lax.axis_index("row"), lax.axis_index("col")
    other_row = 1 - row_id
    me = col_id * row_count + row_id
    side = lax.rem(col_id, 2)
    pair = col_id // 2
    chip = pair * row_count + row_id
    quarters = col_count // 4
    far, quarter = pair // quarters, lax.rem(pair, quarters)
    opposite_col = lax.rem(col_id + span, col_count)
    last = parts - 1
    lane_blocks = [slice(start, start + LANES) for start in range(0, channels, LANES)]

    def loop(first, last, body):
        def one(step, carry):
            body(step)
            return carry

        lax.fori_loop(first, last, one, 0)

    def await_bytes(like, semaphore):
        pltpu.make_async_copy(like, like, semaphore).wait()

    def rows_of(part):
        return pl.ds(part * rows_in_part, rows_in_part)

    def relay_copy(part):
        return pltpu.make_async_remote_copy(
            src_ref=tile_ref.at[:, other_row, rows_of(part)],
            dst_ref=relay_buf.at[part],
            send_sem=relay_send.at[part],
            recv_sem=relay_recv.at[part],
            device_id=(other_row, col_id),
            device_id_type=MESH,
        )

    def start_rows(origin, slot, part, source):
        target = origin * span + slot
        columns = pl.ds(pl.multiple_of(col_id * tile_cols, tile_cols), tile_cols)
        landing = row_buf.at[rows_of(part), columns, :]

        @pl.when(target != col_id)
        def _():
            pltpu.make_async_remote_copy(
                src_ref=source,
                dst_ref=landing,
                send_sem=row_send,
                recv_sem=row_recv.at[part],
                device_id=(row_id, target),
                device_id_type=MESH,
            ).start()

        @pl.when(target == col_id)
        def _():
            pltpu.make_async_copy(source, landing, row_recv.at[part]).start()

    def over_slots(body):
        loop(0, span, lambda step: body(lax.rem(col_id + step, span)))

    def direct(part):
        over_slots(
            lambda slot: start_rows(row_id, slot, part, tile_ref.at[slot, row_id, rows_of(part)])
        )

    def pass_on(part):
        await_bytes(relay_buf.at[part], relay_recv.at[part])
        over_slots(lambda slot: start_rows(other_row, slot, part, relay_buf.at[part, slot]))

    own_columns = pl.ds(pl.multiple_of(row_id * tile_rows, tile_rows), tile_rows)

    def col_remote(part):
        return pltpu.make_async_remote_copy(
            src_ref=turned_ref.at[rows_of(part)],
            dst_ref=col_buf.at[rows_of(part), own_columns, :],
            send_sem=col_send.at[part],
            recv_sem=col_recv.at[part],
            device_id=(other_row, col_id),
            device_id_type=MESH,
        )

    loads = [
        pltpu.make_async_copy(source, target, load_done.at[index])
        for index, (source, target) in enumerate(
            (
                (tile_ref, tile_buf),
                (hidden_weight_hbm, hidden_weight_ref),
                (out_weight_hbm, out_weight_ref),
                (query_weight_hbm, query_weight_ref),
                (key_weight_hbm, key_weight_ref),
                (value_weight_hbm, value_weight_ref),
                (gate_weight_hbm, gate_weight_ref),
                (output_weight_hbm, output_weight_ref),
            )
        )
    ]
    loads[0].start()
    greet_all(row_count, col_count)

    ahead = min(2, parts)
    for part in range(parts):
        relay_copy(part).start()
    for part in range(ahead):
        direct(part)
    loads[0].wait()
    for load in loads[1:]:
        load.start()
    tile_flat = tile_buf.reshape(tile_rows * tile_cols, channels)
    for lane, lanes in enumerate(lane_blocks):
        turned[lane] = tile_flat[:, lanes].astype(jnp.float32)

    def turned_column(column, lane):
        return turned[lane, pl.ds(column, tile_rows, stride=tile_cols), :].astype(jnp.bfloat16)

    for position in range(own):
        for lane, lanes in enumerate(lane_blocks):
            turned_ref[position, :, lanes] = turned_column(other_row * own + position, lane)
    for part in range(parts):
        col_remote(part).start()
    for position in range(own):
        for lane, lanes in enumerate(lane_blocks):
            col_buf[position, own_columns, lanes] = turned_column(row_id * own + position, lane)
    for load in loads[1:]:
        load.wait()
    query_turned[...] = query_weight_ref[...].T
    value_turned[...] = value_weight_ref[...].T
    gate_turned[...] = gate_weight_ref[...].T
    chain_row = jnp.broadcast_to(chain_ref[...].astype(jnp.float32), (length, length))
    same_buf[...] = (chain_row.T == chain_row).astype(jnp.float32)
    penalty_row = mask_penalty * (1 - mask_ref[...]).astype(jnp.float32)
    penalty_buf[...] = jnp.broadcast_to(penalty_row, (length, length)).T

    for part in range(parts):
        pass_on(part)
        if part + ahead < parts:
            direct(part + ahead)

    def bias_piece(part):
        return bias_buf.at[far, quarter, side, row_id, part]

    def quad_copy(part, device):
        return pltpu.make_async_remote_copy(
            src_ref=bias_piece(part),
            dst_ref=bias_piece(part),
            send_sem=quad_send,
            recv_sem=quad_recv.at[part],
            device_id=device,
            device_id_type=MESH,
        )

    def send_quad(part):
        quad_copy(part, (row_id, opposite_col)).start()
        quad_copy(part, (other_row, opposite_col)).start()
        quad_copy(part, (other_row, col_id)).start()

    def pieces(count, rows):
        return recv_buf.at[pl.ds(0, count), pl.ds(0, rows)]

    def send_fan(part):
        await_bytes(pieces(3, rows_in_part), quad_recv.at[part])

        def to_quarter(step):
            target = lax.rem(quarter + step, quarters)
            pltpu.make_async_remote_copy(
                src_ref=bias_buf.at[:, quarter, side, :, part],
                dst_ref=bias_buf.at[:, quarter, side, :, part],
                send_sem=fan_send,
                recv_sem=fan_recv.at[part],
                device_id=(row_id, (far * quarters + target) * 2 + side),
                device_id_type=MESH,
            ).start()

        loop(1, quarters, to_quarter)

    def send_last():
        def to_chip(step):
            other = lax.rem(chip + step, chip_total)
            pltpu.make_async_remote_copy(
                src_ref=bias_piece(last),
                dst_ref=bias_piece(last),
                send_sem=last_send,
                recv_sem=last_recv,
                device_id=(lax.rem(other, row_count), (other // row_count) * 2 + side),
                device_id_type=MESH,
            ).start()

        loop(1, chip_total, to_chip)

    def to_pair(part):
        return pltpu.make_async_remote_copy(
            src_ref=bias_buf.at[:, :, side, :, part],
            dst_ref=bias_buf.at[:, :, side, :, part],
            send_sem=pair_send.at[part],
            recv_sem=pair_recv.at[part],
            device_id=(row_id, col_id + 1 - 2 * side),
            device_id_type=MESH,
        )

    def hand_over(part):
        await_bytes(pieces(4 * (quarters - 1), rows_in_part), fan_recv.at[part])
        to_pair(part).start()

    def transition_row(position):
        sym_row = row_buf[position].astype(jnp.float32) + col_buf[position].astype(jnp.float32)
        first_norm = normalize(sym_row, gain_transition_ref[...]).astype(jnp.bfloat16)
        hidden_act = jax.nn.relu(
            jnp.dot(first_norm, hidden_weight_ref[...], preferred_element_type=jnp.float32)
        ).astype(jnp.bfloat16)
        carried = sym_row + jnp.dot(
            hidden_act, out_weight_ref[...], preferred_element_type=jnp.float32
        )
        carried_buf[position] = carried
        normed = normalize(carried, gain_attention_ref[...]).astype(jnp.bfloat16)
        normed_buf[position] = normed
        part = position // rows_in_part
        bias_buf[far, quarter, side, row_id, part, position - part * rows_in_part] = lax.dot_general(
            bias_weight_ref[...],
            normed,
            (((1,), (1,)), ((), ())),
            preferred_element_type=jnp.float32,
        ).astype(jnp.bfloat16)

    def project_row(position):
        normed = normed_buf[position]
        normed_turned = normed.T

        def project(weight_ref):
            return jnp.dot(weight_ref[...], normed_turned, preferred_element_type=jnp.float32)

        key_buf[position] = jnp.dot(
            normed, key_weight_ref[...], preferred_element_type=jnp.float32
        ).astype(jnp.bfloat16)
        query_buf[position] = project(query_turned).astype(jnp.bfloat16)
        value_buf[position] = project(value_turned).astype(jnp.bfloat16)
        gate_buf[position] = jax.nn.sigmoid(project(gate_turned))

    def await_part(part):
        await_bytes(row_buf.at[rows_of(part)], row_recv.at[part])
        await_bytes(turned_ref.at[rows_of(part)], col_recv.at[part])

    def one_part(part):
        await_part(part)
        loop(part * rows_in_part, (part + 1) * rows_in_part, transition_row)
        send_quad(part)

    loop(0, last, one_part)
    await_part(last)
    early = last * 5 // 8
    loop(0, early, send_fan)
    loop(last * rows_in_part, own, transition_row)
    send_last()
    loop(early, last, send_fan)
    loop(0, own // 2, project_row)
    loop(0, early, hand_over)
    loop(own // 2, own, project_row)
    loop(early, last, hand_over)
    await_bytes(pieces(chip_total - 1, rows_in_part), last_recv)
    to_pair(last).start()
    loop(0, parts, lambda part: await_bytes(bias_buf.at[:, :, side, :, part], pair_recv.at[part]))

    bias_rows = bias_buf.reshape(length * head_count, length)
    for lane, lanes in enumerate(lane_blocks):
        turned[lane] = bias_rows[:, lanes].astype(jnp.float32)
    for head in range(head_count):
        for lane, lanes in enumerate(lane_blocks):
            bias_full[head, :, lanes] = (
                turned[lane, pl.ds(head, length, stride=head_count), :]
                + chain_weight_ref[head] * same_buf[:, lanes]
                - penalty_buf[:, lanes]
            ) * LOG2_E

    strip = min(128, length)
    band = min(inner_total, max(128, head_dim))
    heads_in_band = band // head_dim
    head_of_lane = lax.broadcasted_iota(jnp.int32, (1, band), 1) // head_dim

    def attend_row(position):
        keys, queries, values = key_buf[position], query_buf[position], value_buf[position]

        def score(head):
            first = head // heads_in_band * band
            chosen = (head_of_lane == head % heads_in_band).astype(jnp.bfloat16)
            score_buf[head] = (
                jnp.dot(
                    keys[:, first : first + band] * chosen,
                    queries[first : first + band],
                    preferred_element_type=jnp.float32,
                )
                * score_scale
                + bias_full[head]
            )

        mixed = []
        for head in range(4):
            score(head)
        for head in range(head_count):
            if head + 4 < head_count:
                score(head + 4)
            rows = slice(head * head_dim, (head + 1) * head_dim)
            for start in range(0, length, strip):
                places = slice(start, start + strip)
                scores = score_buf[head, :, places]
                exponent = jnp.exp2(scores - jnp.max(scores, axis=0, keepdims=True))
                weight_buf[head, :, places] = (
                    exponent * (1.0 / jnp.sum(exponent, axis=0, keepdims=True))
                ).astype(jnp.bfloat16)
            mixture = jnp.dot(values[rows], weight_buf[head], preferred_element_type=jnp.float32)
            mixed.append((gate_buf[position, rows] * mixture).astype(jnp.bfloat16))
        gated = jnp.concatenate(mixed, axis=0).T
        update = jnp.dot(gated, output_weight_ref[...], preferred_element_type=jnp.float32)
        update = update.astype(jnp.bfloat16)
        update_buf[position] = update.reshape(device_total, own, channels)
        recv_buf[me, position] = update_buf[position, me]

        def to_peer(step):
            peer = lax.rem(me + step, device_total)
            pltpu.make_async_remote_copy(
                src_ref=update_buf.at[position, peer],
                dst_ref=recv_buf.at[me, position],
                send_sem=update_send,
                recv_sem=update_recv.at[position],
                device_id=(lax.rem(peer, row_count), peer // row_count),
                device_id_type=MESH,
            ).start()

        loop(1, device_total, to_peer)
        total = 2.0 * carried_buf[position] + update.astype(jnp.float32)
        for lane, lanes in enumerate(lane_blocks):
            turned[lane, pl.ds(position, length, stride=own), :] = total[:, lanes]

    loop(0, own, attend_row)

    my_columns = pl.ds(pl.multiple_of(row_id * own, own), own)
    totals = turned.reshape(len(lane_blocks), device_total, own, own, LANES)

    def summed(other, position, lane):
        devices = pl.ds(other * col_count, col_count)
        return (
            totals[lane, devices, position]
            + recv_buf[devices, position, :, lane_blocks[lane]].astype(jnp.float32)
        ).astype(jnp.bfloat16)

    def sum_remote(position):
        return pltpu.make_async_remote_copy(
            src_ref=sum_buf.at[:, position],
            dst_ref=out_ref.at[:, position, my_columns],
            send_sem=sum_send.at[position],
            recv_sem=sum_recv.at[position],
            device_id=(other_row, col_id),
            device_id_type=MESH,
        )

    def finish_position(position):
        await_bytes(recv_buf.at[pl.ds(0, device_total - 1), position], update_recv.at[position])
        for lane, lanes in enumerate(lane_blocks):
            sum_buf[:, position, :, lanes] = summed(other_row, position, lane)
        sum_remote(position).start()
        for lane, lanes in enumerate(lane_blocks):
            out_ref[:, position, my_columns, lanes] = summed(row_id, position, lane)

    loop(0, own, finish_position)

    await_bytes(recv_buf.at[pl.ds(0, device_total - 1)], update_send)
    await_bytes(pieces(3, last * rows_in_part), quad_send)
    await_bytes(pieces(4 * (quarters - 1), last * rows_in_part), fan_send)
    await_bytes(pieces(chip_total - 1, rows_in_part), last_send)
    await_bytes(row_buf.at[:, pl.ds(0, length - tile_cols)], row_send)

    def close_part(part):
        relay_copy(part).wait_send()
        col_remote(part).wait_send()
        to_pair(part).wait_send()

    loop(0, parts, close_part)

    def close_position(position):
        await_bytes(sum_buf.at[:, position], sum_recv.at[position])
        sum_remote(position).wait_send()

    loop(0, own, close_position)


def owned_columns(
    pair_state,
    residue_mask,
    chain_ids,
    gain_transition,
    hidden_weight,
    out_weight,
    gain_attention,
    query_weight,
    key_weight,
    value_weight,
    gate_weight,
    bias_weight,
    chain_weight,
    output_weight,
):
    tile_rows, tile_cols, channels = pair_state.shape
    row_count, col_count = lax.axis_size("row"), lax.axis_size("col")
    device_total = row_count * col_count
    head_count = chain_weight.shape[0]
    inner_total = key_weight.shape[1]
    length = tile_rows * row_count
    own = tile_cols // row_count
    span = col_count // row_count
    parts = PARTS
    rows_in_part = own // parts
    in_vmem = pl.BlockSpec(memory_space=pltpu.VMEM)
    in_hbm = pl.BlockSpec(memory_space=pl.ANY)
    in_smem = pl.BlockSpec(memory_space=pltpu.SMEM)
    dma = pltpu.SemaphoreType.DMA

    def half(*shape):
        return pltpu.VMEM(shape, jnp.bfloat16)

    def full(*shape):
        return pltpu.VMEM(shape, jnp.float32)

    out = pl.pallas_call(
        functools.partial(layer_kernel, row_count, col_count),
        out_shape=jax.ShapeDtypeStruct((col_count, own, tile_cols, channels), jnp.bfloat16),
        in_specs=[
            in_hbm,
            in_vmem,
            in_vmem,
            in_vmem,
            in_hbm,
            in_hbm,
            in_vmem,
            in_hbm,
            in_hbm,
            in_hbm,
            in_hbm,
            in_vmem,
            in_smem,
            in_hbm,
        ],
        out_specs=in_vmem,
        scratch_shapes=[
            half(span, row_count, own, tile_cols, channels),
            half(*hidden_weight.shape),
            half(*out_weight.shape),
            half(*query_weight.shape),
            half(*key_weight.shape),
            half(*value_weight.shape),
            half(*gate_weight.shape),
            half(*output_weight.shape),
            half(own, length, channels),
            half(own, length, channels),
            half(own, tile_rows, channels),
            half(parts, span, rows_in_part, tile_cols, channels),
            half(2, col_count // 4, 2, row_count, parts, rows_in_part, head_count, length),
            full(length, length),
            full(length, length),
            full(head_count, length, length),
            full(own, length, channels),
            half(own, length, channels),
            half(own, length, inner_total),
            half(own, inner_total, length),
            half(own, inner_total, length),
            full(own, inner_total, length),
            half(*query_weight.shape[::-1]),
            half(*value_weight.shape[::-1]),
            half(*gate_weight.shape[::-1]),
            full(head_count, length, length),
            half(head_count, length, length),
            half(own, device_total, own, channels),
            half(device_total, own, own, channels),
            full(channels // LANES, length * own, LANES),
            half(col_count, own, own, channels),
            dma((8,)),
            dma((parts,)),
            dma((parts,)),
            dma,
            dma((parts,)),
            dma((parts,)),
            dma((parts,)),
            dma,
            dma((parts,)),
            dma,
            dma((parts,)),
            dma,
            dma,
            dma((parts,)),
            dma((parts,)),
            dma,
            dma((own,)),
            dma((own,)),
            dma((own,)),
        ],
        compiler_params=pltpu.CompilerParams(
            collective_id=0, has_side_effects=True, vmem_limit_bytes=VMEM_LIMIT
        ),
        name="layer",
    )(
        pair_state.reshape(span, row_count, own, tile_cols, channels),
        residue_mask[None, :],
        chain_ids[None, :],
        gain_transition[None, :],
        hidden_weight,
        out_weight,
        gain_attention[None, :],
        query_weight,
        key_weight,
        value_weight,
        gate_weight,
        bias_weight.T,
        chain_weight,
        output_weight,
    )
    return out.reshape(tile_rows, tile_cols, channels)


def per_device(pair_state, *others):
    tile_cols = pair_state.shape[1]
    row_count, col_count = lax.axis_size("row"), lax.axis_size("col")
    own = tile_cols // row_count
    length = row_count * pair_state.shape[0]
    fits = own == 8 and row_count == 2 and col_count % 4 == 0
    fits = fits and length == pair_state.shape[2] and length % LANES == 0
    if fits and others[11].shape[0] == own and pair_state.shape[0] == col_count * own:
        return owned_columns(pair_state, *others)
    return tile_layout(pair_state, *others)


def solution(mesh):
    placed = (
        P("row", "col", None),
        P(),
        P(),
        P(),
        P(),
        P(),
        P(),
        P(),
        P(),
        P(),
        P(),
        P(),
        P(),
        P(),
    )
    return jax.shard_map(
        per_device, mesh=mesh, in_specs=placed, out_specs=P("row", "col", None), check_vma=False
    )
```
